1024 devices in a mesh: dp: 64 (over x, z), ctx: 16 (over y, core).
Axes of the slice: x: 8, y: 8, z: 8, core: 2. Of those that a mesh axis runs over, the one named last changes fastest.
Arguments:
- queries: bfloat16 [64, 16, 2, 64, 2048], P('dp', 'ctx'), may hold values from -6 to 6
- keys: bfloat16 [64, 16, 2, 64, 512], P('dp', 'ctx'), may hold values from -6 to 6
- values: bfloat16 [64, 16, 2, 64, 512], P('dp', 'ctx'), may hold values from -6 to 6
- out_grad: bfloat16 [64, 16, 2, 64, 2048], P('dp', 'ctx'), may hold values from -6 to 6
- layer_input: bfloat16 [64, 16, 2, 64, 4096], P('dp', 'ctx'), may hold values from -6 to 6
- doc_lengths: int32 [64, 64], P('dp'), may hold values from 1 to 64, as said below
Outputs:
- query_grad: bfloat16 [64, 16, 2, 64, 2048], P('dp', 'ctx')
- key_grad: bfloat16 [64, 16, 2, 64, 512], P('dp', 'ctx')
- value_grad: bfloat16 [64, 16, 2, 64, 512], P('dp', 'ctx')
- weight_grad: float32 [4096, 512], P('ctx', 'dp')
The draws below stay inside these ranges and needn't reach their ends.
Inputs may be any that keep to these rules, and one draw needn't show every extreme that they name: `doc_lengths`: each sequence is 64 documents laid end to end that fill its 2048 tokens; no document is longer than 64 tokens, and one of each sequence has exactly 64.
All inputs are finite; a program needn't handle non-finite values.
Results may differ from the reference program's by a relative error of at most 0.03.
Values may be sent and summed in bfloat16 or wider, within the bound.
No kernel may reach another device: no remote copies, remote signals or barrier semaphores. Data moves between devices by JAX's collectives and lax.ppermute only.
A program may use at most 32 MiB of HBM per device.

```python
import math
import jax
import jax.numpy as jnp
from jax import lax

HQ = 16
KVH = 4
HD = 128
D = 4096
STRETCH = 64
PAIRS = 16
SEQS = 64
SEQ = 2048


def doc_layout(key):
    base_key = jax.random.fold_in(key, 17)
    offset_key, pick_key = jax.random.split(base_key)
    spans_count = 2 * PAIRS
    index_row = jnp.arange(spans_count, dtype=jnp.int32)[None, :]
    offsets = jax.random.randint(offset_key, (SEQS, spans_count), 1, STRETCH).astype(jnp.int32)
    offsets = jnp.where(index_row == spans_count - 1, jnp.minimum(offsets, STRETCH - 2), offsets)
    offsets = jnp.where(index_row == 0, 0, offsets)
    anchors = index_row * STRETCH + offsets
    ends = jnp.concatenate([anchors[:, 1:], jnp.full((SEQS, 1), SEQ, jnp.int32)], axis=1)
    spans = ends - anchors
    lowest = jnp.maximum(1, spans - STRETCH)
    highest = jnp.minimum(STRETCH, spans - 1)
    picks = jax.random.randint(pick_key, (SEQS, spans_count), 0, 1 << 20).astype(jnp.int32)
    cuts = lowest + picks % (highest - lowest + 1)
    cuts = jnp.where(index_row == 0, STRETCH, cuts)
    lengths = jnp.stack([cuts, spans - cuts], axis=2).reshape(SEQS, 2 * spans_count)
    return lengths.astype(jnp.int32)


def to_slots(natural):
    lower = natural[:, :PAIRS]
    upper = natural[:, PAIRS:][:, ::-1]
    return jnp.stack([lower, upper], axis=2)


def draw_doc_lengths(key, part):
    return doc_layout(key)


def draw_queries(key, part):
    group_size = HQ // KVH
    shape = (SEQS, SEQ, KVH, group_size, HD)
    query_key = jax.random.fold_in(key, 31)
    base = jax.random.truncated_normal(query_key, -4.0, 4.0, shape)
    natural = base.reshape(SEQS, 2 * PAIRS, STRETCH, HQ * HD)
    return to_slots(natural).astype(jnp.bfloat16)


def draw_keys(key, part):
    shape = (SEQS, SEQ, KVH, HD)
    key_key = jax.random.fold_in(key, 37)
    base = jax.random.truncated_normal(key_key, -4.0, 4.0, shape)
    natural = base.reshape(SEQS, 2 * PAIRS, STRETCH, KVH * HD)
    return to_slots(natural).astype(jnp.bfloat16)


def spiked(values, rng, source, target, parts, factor):
    owner, partner = [(jnp.arange(values.shape[dim]) // (values.shape[dim] // parts)).reshape([-1 if axis == dim else 1 for axis in range(values.ndim)]) for dim in (source, target)]
    chosen = jax.random.permutation(rng, parts)[partner]
    strong = (owner == chosen) | (owner == (partner + parts // 2) % parts)
    return jnp.where(strong, factor * values, values)


def level_of(rng, shape, cuts, low, largest):
    def one(dim, blocks):
        steps = jax.random.uniform(jax.random.fold_in(jax.random.fold_in(rng, 6), dim), (blocks,), jnp.float32, low / len(cuts), largest / len(cuts))
        return jnp.repeat(jnp.exp(steps), shape[dim] // blocks).reshape((-1,) + (1,) * (len(shape) - dim - 1))

    gain = one(*cuts[0])
    for cut in cuts[1:]:
        gain = gain * one(*cut)
    return gain


def gaussian(rng, shape, scale, bound, cuts=(), kind=jnp.bfloat16):
    result = scale * jax.random.normal(rng, shape, jnp.float32)
    if cuts:
        result = result * level_of(rng, shape, cuts, -0.22, 0.18)
    return jnp.clip(result, -bound, bound).astype(kind)


def heavy_noise(own_key, shape, width, limit, cuts, heavy, held_as=jnp.bfloat16):
    values = width * jax.random.normal(own_key, shape, jnp.float32)
    if cuts:
        values = values * level_of(own_key, shape, cuts, -0.22, 0.18)
    return jnp.clip(spiked(values, jax.random.fold_in(own_key, 3), *heavy), -limit, limit).astype(held_as)


def setup_inputs(seed: int = 0) -> dict:
    key_of = jax.random.split(jax.random.key(seed), 7)
    queries = draw_queries(jax.random.fold_in(key_of[6], 71), 0)
    keys = draw_keys(jax.random.fold_in(key_of[6], 71), 0)
    values = gaussian(key_of[2], (SEQS, PAIRS, 2, STRETCH, KVH * HD), 1.0, 6.0, ((0, 64), (1, 16)))
    out_grad = gaussian(key_of[3], (SEQS, PAIRS, 2, STRETCH, HQ * HD), 1.0, 6.0, ((0, 64), (1, 16)))
    layer_input = heavy_noise(key_of[4], (SEQS, PAIRS, 2, STRETCH, D), 1.0, 6.0, ((0, 64), (1, 16)), (1, 4, 16, 2.0))
    doc_lengths = draw_doc_lengths(jax.random.fold_in(key_of[6], 71), 0)
    return {"queries": queries, "keys": keys, "values": values, "out_grad": out_grad, "layer_input": layer_input, "doc_lengths": doc_lengths}


def doc_index(starts, positions):
    return (lax.optimization_barrier(jnp.sum((starts <= positions[..., None]).astype(jnp.int32), axis=-1)) - 1).astype(jnp.int32)

def attend(query_rows, key_block, value_block, grad_rows, query_pos, key_pos, starts):
    blocks, rows, query_width = query_rows.shape
    columns = key_block.shape[1]
    kv_heads = key_block.shape[2] // HD
    groups = query_width // HD // kv_heads
    inverse_root = 1.0 / math.sqrt(HD)
    query_heads = query_rows.reshape(blocks, rows, kv_heads, groups, HD).astype(jnp.float32)
    grad_heads = grad_rows.reshape(blocks, rows, kv_heads, groups, HD).astype(jnp.float32)
    key_heads = key_block.reshape(blocks, columns, kv_heads, HD).astype(jnp.float32)
    value_heads = value_block.reshape(blocks, columns, kv_heads, HD).astype(jnp.float32)
    query_doc = doc_index(starts, query_pos)
    key_doc = doc_index(starts, key_pos)
    allowed = (query_doc[:, :, None] == key_doc[:, None, :]) & (key_pos[:, None, :] <= query_pos[:, :, None]) & (key_pos[:, None, :] >= 0)
    scores = jnp.einsum('bqngd,bknd->bngqk', query_heads, key_heads) * inverse_root
    scores = jnp.where(allowed[:, None, None], scores, -1e+30)
    top_score = lax.optimization_barrier(jnp.max(scores, axis=-1, keepdims=True))
    log_total = top_score + jnp.log(lax.optimization_barrier(jnp.sum(jnp.exp(scores - top_score), axis=-1, keepdims=True)))
    probs = jnp.exp(scores - log_total)
    probs_low = probs.astype(jnp.bfloat16)
    attn_out = jnp.einsum('bngqk,bknd->bqngd', probs_low.astype(jnp.float32), value_heads).astype(jnp.bfloat16)
    delta = lax.optimization_barrier(jnp.sum(grad_heads * attn_out.astype(jnp.float32), axis=-1))
    dprob = jnp.einsum('bqngd,bknd->bngqk', grad_heads, value_heads)
    dscore = (probs * (dprob - jnp.transpose(delta, (0, 2, 3, 1))[..., None])).astype(jnp.bfloat16)
    dscore_wide = dscore.astype(jnp.float32)
    query_grad = (jnp.einsum('bngqk,bknd->bqngd', dscore_wide, key_heads) * inverse_root).astype(jnp.bfloat16)
    key_terms = jnp.einsum('bngqk,bqngd->bknd', dscore_wide, query_heads) * inverse_root
    value_terms = jnp.einsum('bngqk,bqngd->bknd', probs_low.astype(jnp.float32), grad_heads)
    return (query_grad.reshape(blocks, rows, query_width), key_terms.reshape(blocks, columns, kv_heads * HD), value_terms.reshape(blocks, columns, kv_heads * HD))

def natural_order(slots):
    return jnp.concatenate([slots[:, 0], slots[::-1, 1]], axis=0)

def slot_order(natural):
    return jnp.stack([natural[:PAIRS], natural[PAIRS:][::-1]], axis=1)

def one_sequence(inputs):
    query_slots, key_slots, value_slots, grad_slots, lengths = inputs
    starts = (jnp.cumsum(lengths) - lengths).astype(jnp.int32)
    query_rows = natural_order(query_slots)
    key_rows = natural_order(key_slots)
    value_rows = natural_order(value_slots)
    grad_rows = natural_order(grad_slots)
    empty_block = jnp.zeros_like(key_rows[:1])
    key_block = jnp.concatenate([jnp.concatenate([empty_block, key_rows[:-1]], axis=0), key_rows], axis=1)
    value_block = jnp.concatenate([jnp.concatenate([empty_block, value_rows[:-1]], axis=0), value_rows], axis=1)
    stretch_ids = jnp.arange(2 * PAIRS, dtype=jnp.int32)
    offsets = jnp.arange(STRETCH, dtype=jnp.int32)
    query_pos = (stretch_ids[:, None] * STRETCH + offsets[None, :]).astype(jnp.int32)
    key_pos = jnp.concatenate([query_pos - STRETCH, query_pos], axis=1).astype(jnp.int32)
    query_grad, key_terms, value_terms = attend(query_rows, key_block, value_block, grad_rows, query_pos, key_pos, starts)
    tail_zero = jnp.zeros((1, STRETCH, key_terms.shape[2]), jnp.float32)
    key_grad = key_terms[:, STRETCH:] + jnp.concatenate([key_terms[1:, :STRETCH], tail_zero], axis=0)
    value_grad = value_terms[:, STRETCH:] + jnp.concatenate([value_terms[1:, :STRETCH], tail_zero], axis=0)
    return (slot_order(query_grad), slot_order(key_grad.astype(jnp.bfloat16)), slot_order(value_grad.astype(jnp.bfloat16)))

def reference(queries, keys, values, out_grad, layer_input, doc_lengths):
    query_grad, key_grad, value_grad = lax.map(one_sequence, (queries, keys, values, out_grad, doc_lengths))
    flat_input = layer_input.reshape(SEQS * PAIRS, 2 * STRETCH, D)
    flat_values = value_grad.reshape(SEQS * PAIRS, 2 * STRETCH, KVH * HD)

    def accumulate(total, pieces):
        input_rows, value_rows = pieces
        partial_value = jnp.dot(input_rows.T, value_rows, preferred_element_type=jnp.float32).astype(jnp.bfloat16)
        partial_value = lax.optimization_barrier(partial_value)
        return (total + partial_value.astype(jnp.float32), None)
    total = lax.scan(accumulate, jnp.zeros((D, KVH * HD), jnp.float32), (flat_input, flat_values))[0]
    weight_grad = total / jnp.float32(SEQS)
    return (query_grad, key_grad, value_grad, weight_grad)
```

```python
import math

import jax
import jax.numpy as jnp
from jax import lax
from jax.experimental import pallas as pl
from jax.experimental.pallas import tpu as pltpu
from jax.sharding import Mesh, PartitionSpec as P

HD = 128
NEG = -1e30


def shift_along(value, axis, steps):
    count = lax.axis_size(axis)
    first, last = (max(0, -steps), min(count, count - steps))
    return lax.ppermute(value, axis, [(source, source + steps) for source in range(first, last)])


def contract(left, right, dims):
    return lax.dot_general(left, right, (dims, ((), ())), preferred_element_type=jnp.float32)


def attend_kernel(
    place_ref, lengths_ref, q_ref, k_ref, v_ref, g_ref, halo_lo_ref, halo_hi_ref,
    dq_ref, own_ref, halo_ref,
):
    rows = k_ref.shape[1]
    kv_heads = k_ref.shape[2] // HD
    groups = q_ref.shape[2] // HD // kv_heads
    docs = lengths_ref.shape[1]
    place = place_ref[0]
    last = place_ref[1]
    inverse_root = 1.0 / math.sqrt(HD)
    lengths = jnp.broadcast_to(lengths_ref[...], (docs, docs))
    before = lax.broadcasted_iota(jnp.int32, (docs, docs), 1) < lax.broadcasted_iota(
        jnp.int32, (docs, docs), 0
    )
    starts = jnp.sum(
        jnp.where(before, lengths, 0).astype(jnp.float32), axis=1, keepdims=True
    )
    columns = groups * rows
    for slot in range(2):
        base = place * rows if slot == 0 else (2 * last + 1 - place) * rows
        lane = lax.broadcasted_iota(jnp.int32, (docs, columns), 1)
        query_pos = (base + lax.rem(lane, rows)).astype(jnp.float32)
        first_key = jnp.max(
            jnp.where(starts <= query_pos, starts, -1.0), axis=0, keepdims=True
        )
        key_pos = (base - rows + lax.broadcasted_iota(jnp.int32, (2 * rows, columns), 0)).astype(
            jnp.float32
        )
        allowed = (key_pos >= first_key) & (key_pos <= query_pos[:1])
        for head in range(kv_heads):
            at = slice(head * HD, (head + 1) * HD)
            if slot == 0:
                key_prev, value_prev = halo_lo_ref[0, :, at], halo_lo_ref[1, :, at]
            else:
                key_prev = jnp.where(place == last, k_ref[0, :, at], halo_hi_ref[0, :, at])
                value_prev = jnp.where(place == last, v_ref[0, :, at], halo_hi_ref[1, :, at])
            key = jnp.concatenate([key_prev, k_ref[slot, :, at]], axis=0)
            value = jnp.concatenate([value_prev, v_ref[slot, :, at]], axis=0)
            wide = [
                slice((head * groups + member) * HD, (head * groups + member + 1) * HD)
                for member in range(groups)
            ]
            query = jnp.concatenate([q_ref[slot, :, one] for one in wide], axis=0)
            grad = jnp.concatenate([g_ref[slot, :, one] for one in wide], axis=0)
            scores = contract(key, query, ((1,), (1,))) * inverse_root
            scores = jnp.where(allowed, scores, NEG)
            top = jnp.max(scores, axis=0, keepdims=True)
            weight = jnp.exp(scores - top)
            probs = weight * (1.0 / jnp.sum(weight, axis=0, keepdims=True))
            probs_low = probs.astype(jnp.bfloat16)
            dprob = contract(value, grad, ((1,), (1,)))
            delta = jnp.sum(probs_low.astype(jnp.float32) * dprob, axis=0, keepdims=True)
            dscore = (probs * (dprob - delta)).astype(jnp.bfloat16)
            query_grad = (contract(dscore, key, ((0,), (0,))) * inverse_root).astype(jnp.bfloat16)
            for member, one in enumerate(wide):
                dq_ref[slot, :, one] = query_grad[member * rows : (member + 1) * rows]
            key_grad = contract(dscore, query, ((1,), (0,))) * inverse_root
            value_grad = contract(probs_low, grad, ((1,), (0,)))
            halo_ref[slot, 0, :, at] = key_grad[:rows].astype(jnp.bfloat16)
            halo_ref[slot, 1, :, at] = value_grad[:rows].astype(jnp.bfloat16)
            own_ref[slot, 0, :, at] = key_grad[rows:]
            own_ref[slot, 1, :, at] = value_grad[rows:]
            if slot == 1:
                own_ref[0, 0, :, at] += jnp.where(place == last, key_grad[:rows], 0.0)
                own_ref[0, 1, :, at] += jnp.where(place == last, value_grad[:rows], 0.0)


def attend(place, lengths, q, k, v, g, halo_lo, halo_hi):
    rows, width = k.shape[1:]
    vmem = pl.BlockSpec(memory_space=pltpu.VMEM)
    return pl.pallas_call(
        attend_kernel,
        name="attend",
        in_specs=[pl.BlockSpec(memory_space=pltpu.SMEM)] + [vmem] * 7,
        out_specs=[vmem] * 3,
        out_shape=[
            jax.ShapeDtypeStruct(q.shape, jnp.bfloat16),
            jax.ShapeDtypeStruct((2, 2, rows, width), jnp.float32),
            jax.ShapeDtypeStruct((2, 2, rows, width), jnp.bfloat16),
        ],
    )(place, lengths, q, k, v, g, halo_lo, halo_hi)


CTX = ("y", "core")


def body(queries, keys, values, out_grad, layer_input, doc_lengths):
    k, v = keys[0, 0], values[0, 0]
    ctx = lax.axis_size(CTX)
    place = jnp.stack([lax.axis_index(CTX), jnp.int32(ctx - 1)]).astype(jnp.int32)
    halo_lo = shift_along(jnp.stack([k[0], v[0]]), CTX, 1)
    halo_hi = shift_along(jnp.stack([k[1], v[1]]), CTX, -1)
    query_grad, own, halo = attend(
        place, doc_lengths, queries[0, 0], k, v, out_grad[0, 0], halo_lo, halo_hi
    )
    came = jnp.stack([shift_along(halo[0], CTX, -1), shift_along(halo[1], CTX, 1)])
    total = (own + came.astype(jnp.float32)).astype(jnp.bfloat16)
    key_grad, value_grad = total[:, 0], total[:, 1]
    tokens = 2 * k.shape[1]
    width = k.shape[2]
    depth = layer_input.shape[4]
    rows = depth // ctx
    inputs = layer_input[0, 0].reshape(tokens, ctx, rows).transpose(1, 0, 2)
    inputs = lax.all_to_all(inputs, CTX, 0, 0, tiled=True).reshape(ctx * tokens, rows)
    gathered = lax.all_gather(value_grad.reshape(tokens, width), CTX, axis=0, tiled=True)
    block = contract(gathered, inputs, ((0,), (0,)))
    for axis in ("x", "z"):
        count = lax.axis_size(axis)
        parts = block.astype(jnp.bfloat16).reshape(count, block.shape[0] // count, rows)
        parts = lax.all_to_all(parts, axis, 0, 0, tiled=True)
        block = jnp.sum(parts.astype(jnp.float32), axis=0)
    seqs = lax.axis_size(("x", "z"))
    weight_grad = block.T / jnp.float32(seqs)
    return (query_grad[None, None], key_grad[None, None], value_grad[None, None], weight_grad)


def solution(mesh):
    devices = mesh.devices
    side = math.isqrt(devices.shape[0])
    split = Mesh(devices.reshape(side, side, devices.shape[1] // 2, 2), ("x", "z", "y", "core"))
    dp, ctx = ("x", "z"), CTX
    slots = P(dp, ctx, None, None, None)
    return jax.shard_map(
        body,
        mesh=split,
        in_specs=(slots,) * 5 + (P(dp, None),),
        out_specs=(slots, slots, slots, P(ctx, dp)),
        check_vma=False,
    )
```

```python
import functools
import math

import jax
import jax.numpy as jnp
from jax import lax
from jax.experimental import pallas as pl
from jax.experimental.pallas import tpu as pltpu
from jax.sharding import Mesh, PartitionSpec as P


HD = 128
NEG = -1e30


def shift_along(value, axis, steps):
    count = lax.axis_size(axis)
    first, last = (max(0, -steps), min(count, count - steps))
    return lax.ppermute(value, axis, [(source, source + steps) for source in range(first, last)])


def contract(left, right, dims):
    return lax.dot_general(left, right, (dims, ((), ())), preferred_element_type=jnp.float32)


def attend_kernel(
    place_ref, lengths_ref, q_ref, k_ref, v_ref, g_ref, halo_lo_ref, halo_hi_ref,
    dq_ref, own_ref, send_lo_ref, send_hi_ref, *, last,
):
    rows = k_ref.shape[1]
    kv_heads = k_ref.shape[2] // HD
    groups = q_ref.shape[2] // HD // kv_heads
    docs = lengths_ref.shape[1]
    place = place_ref[0]
    inverse_root = 1.0 / math.sqrt(HD)
    lengths = jnp.broadcast_to(lengths_ref[...], (docs, docs))
    before = lax.broadcasted_iota(jnp.int32, (docs, docs), 1) < lax.broadcasted_iota(
        jnp.int32, (docs, docs), 0
    )
    starts = jnp.sum(
        jnp.where(before, lengths, 0).astype(jnp.float32), axis=1, keepdims=True
    )
    columns = groups * rows
    for slot in range(2):
        base = place * rows if slot == 0 else (2 * last + 1 - place) * rows
        lane = lax.broadcasted_iota(jnp.int32, (docs, columns), 1)
        query_pos = (base + lax.rem(lane, rows)).astype(jnp.float32)
        first_key = jnp.max(
            jnp.where(starts <= query_pos, starts, -1.0), axis=0, keepdims=True
        )
        key_pos = (base - rows + lax.broadcasted_iota(jnp.int32, (2 * rows, columns), 0)).astype(
            jnp.float32
        )
        allowed = (key_pos >= first_key) & (key_pos <= query_pos[:1])
        for head in range(kv_heads):
            at = slice(head * HD, (head + 1) * HD)
            if slot == 0:
                key_prev, value_prev = halo_lo_ref[0, :, at], halo_lo_ref[1, :, at]
            else:
                key_prev = jnp.where(place == last, k_ref[0, :, at], halo_hi_ref[0, :, at])
                value_prev = jnp.where(place == last, v_ref[0, :, at], halo_hi_ref[1, :, at])
            key = jnp.concatenate([key_prev, k_ref[slot, :, at]], axis=0)
            value = jnp.concatenate([value_prev, v_ref[slot, :, at]], axis=0)
            wide = [
                slice((head * groups + member) * HD, (head * groups + member + 1) * HD)
                for member in range(groups)
            ]
            query = jnp.concatenate([q_ref[slot, :, one] for one in wide], axis=0)
            grad = jnp.concatenate([g_ref[slot, :, one] for one in wide], axis=0)
            scores = contract(key, query, ((1,), (1,))) * inverse_root
            scores = jnp.where(allowed, scores, NEG)
            top = jnp.max(scores, axis=0, keepdims=True)
            weight = jnp.exp(scores - top)
            probs = weight * (1.0 / jnp.sum(weight, axis=0, keepdims=True))
            probs_low = probs.astype(jnp.bfloat16)
            dprob = contract(value, grad, ((1,), (1,)))
            delta = jnp.sum(probs_low.astype(jnp.float32) * dprob, axis=0, keepdims=True)
            dscore = (probs * (dprob - delta)).astype(jnp.bfloat16)
            query_grad = (contract(dscore, key, ((0,), (0,))) * inverse_root).astype(jnp.bfloat16)
            for member, one in enumerate(wide):
                dq_ref[slot, :, one] = query_grad[member * rows : (member + 1) * rows]
            key_grad = contract(dscore, query, ((1,), (0,))) * inverse_root
            value_grad = contract(probs_low, grad, ((1,), (0,)))
            halo_ref = send_hi_ref if slot else send_lo_ref
            halo_ref[0, :, at] = key_grad[:rows].astype(jnp.bfloat16)
            halo_ref[1, :, at] = value_grad[:rows].astype(jnp.bfloat16)
            own_ref[slot, 0, :, at] = key_grad[rows:]
            own_ref[slot, 1, :, at] = value_grad[rows:]
            if slot == 1:
                own_ref[0, 0, :, at] += jnp.where(place == last, key_grad[:rows], 0.0)
                own_ref[0, 1, :, at] += jnp.where(place == last, value_grad[:rows], 0.0)


def whole(kernel, name, out_shape, scratch=()):
    vmem = pl.BlockSpec(memory_space=pltpu.VMEM)

    def call(place, *arrays):
        if name == "finish":
            arrays = [pltpu.with_memory_space_constraint(one, pltpu.VMEM) for one in arrays]
        return pl.pallas_call(
            kernel,
            in_specs=[pl.BlockSpec(memory_space=pltpu.SMEM)] + [vmem] * len(arrays),
            out_specs=[vmem] * len(out_shape),
            out_shape=out_shape,
            scratch_shapes=scratch,
        )(place, *arrays)

    return call


def like(shape, dtype):
    return jax.ShapeDtypeStruct(shape, dtype)


def finish_kernel(place_ref, own_ref, came_lo_ref, came_hi_ref, key_ref, value_ref):
    for slot, came_ref in ((0, came_lo_ref), (1, came_hi_ref)):
        for kind, out_ref in ((0, key_ref), (1, value_ref)):
            total = own_ref[slot, kind] + came_ref[kind].astype(jnp.float32)
            out_ref[slot] = total.astype(jnp.bfloat16)


def outer_kernel(place_ref, *refs):
    *in_refs, keep_ref, send_ref, total_ref = refs
    count = len(in_refs) // 2
    for step in range(count):
        part = contract(in_refs[step][...], in_refs[count + step][...], ((0,), (0,)))
        total_ref[...] = part if step == 0 else total_ref[...] + part
    half = keep_ref.shape[1]
    core = lax.rem(place_ref[0], 2)
    keep_ref[...] = total_ref[:, pl.ds(pl.multiple_of(core * half, half), half)]
    other = total_ref[:, pl.ds(pl.multiple_of((1 - core) * half, half), half)]
    send_ref[...] = other.astype(send_ref.dtype)


CTX = ("y", "core")
DP = ("x", "z")


def body(queries, keys, values, out_grad, layer_input, doc_lengths):
    q, k, v, g = queries[0, 0], keys[0, 0], values[0, 0], out_grad[0, 0]
    ctx, seqs, ring = lax.axis_size(CTX), lax.axis_size(DP), lax.axis_size("y")
    place = jnp.stack([lax.axis_index(CTX), lax.axis_index(DP)]).astype(jnp.int32)
    rows, width = k.shape[1:]
    tokens = 2 * rows
    depth = layer_input.shape[4]
    share = depth // ring
    half = depth // ctx
    halo_lo = shift_along(jnp.stack([k[0], v[0]]), CTX, 1)
    halo_hi = shift_along(jnp.stack([k[1], v[1]]), CTX, -1)
    query_grad, own, send_lo, send_hi = whole(
        functools.partial(attend_kernel, last=ctx - 1),
        "attend",
        [
            like(q.shape, jnp.bfloat16),
            like((2, 2, rows, width), jnp.float32),
            like((2, rows, width), jnp.bfloat16),
            like((2, rows, width), jnp.bfloat16),
        ],
    )(place, doc_lengths, q, k, v, g, halo_lo, halo_hi)
    came_lo = shift_along(send_lo, CTX, -1)
    came_hi = shift_along(send_hi, CTX, 1)
    key_grad, value_grad = whole(finish_kernel, "finish", [like(k.shape, jnp.bfloat16)] * 2)(
        place, own, came_lo, came_hi
    )
    flat = value_grad.reshape(tokens, width)
    inputs = layer_input[0, 0].reshape(tokens, ring, share).transpose(1, 0, 2)
    inputs = lax.all_to_all(inputs, "y", 0, 0, tiled=True).reshape(ring * tokens, share)
    copies = jnp.broadcast_to(flat[None], (ring, tokens, width))
    gathered = lax.all_to_all(copies, "y", 0, 0, tiled=True).reshape(ring * tokens, width)
    keep, send = whole(
        outer_kernel,
        "outer",
        [like((width, half), jnp.float32), like((width, half), jnp.bfloat16)],
        [pltpu.VMEM((width, share), jnp.float32)],
    )(place, gathered, inputs)
    block = keep + lax.ppermute(send, "core", [(0, 1), (1, 0)]).astype(jnp.float32)
    for axis in DP:
        count = lax.axis_size(axis)
        parts = block.astype(jnp.bfloat16).reshape(count, block.shape[0] // count, half)
        parts = lax.all_to_all(parts, axis, 0, 0, tiled=True)
        block = jnp.sum(parts.astype(jnp.float32), axis=0)
    weight_grad = block.T / jnp.float32(seqs)
    return (query_grad[None, None], key_grad[None, None], value_grad[None, None], weight_grad)


def solution(mesh):
    devices = mesh.devices
    side = math.isqrt(devices.shape[0])
    split = Mesh(devices.reshape(side, side, devices.shape[1] // 2, 2), DP + CTX)
    slots = P(DP, CTX, None, None, None)

    return jax.shard_map(
        body,
        mesh=split,
        in_specs=(slots,) * 5 + (P(DP, None),),
        out_specs=(slots, slots, slots, P(CTX, DP)),
        check_vma=False,
    )
```
